512 devices in a mesh: depth: 8 (over y), tile: 64 (over x, z, core).
Axes of the slice: x: 4, y: 8, z: 8, core: 2. Of those that a mesh axis runs over, the one named last changes fastest.
Arguments:
- residual: float32 [65536], P(('depth', 'tile')), may hold values from -15 to 15
- ray_event: int32 [65536], P(('depth', 'tile')), may hold values from 0 to 15, as said below
- ray_owner: int32 [65536, 4], P(('depth', 'tile')), may hold values from 0 to 511, all different within a row; in each aligned block of 128 rows (0 to 127, 128 to 255, ...) at most 2 rows name the same one
- ray_patch: int32 [65536, 4], P(('depth', 'tile')), may hold values from 0 to 31
- tube_center: float32 [2, 65536, 4], P(None, ('depth', 'tile')), may hold values from 0 to 1
- tube_tilt: float32 [2, 65536, 4], P(None, ('depth', 'tile')), may hold values from -0.5 to 0.5
- fresnel: float32 [128], replicated, may hold values from 2 to 16
- radial_width: float32 [128], replicated, may hold values from 1 to 8
Outputs:
- smoothed: float32 [64, 4096, 128], P('tile', 'depth')
The draws below stay inside these ranges and needn't reach their ends.
Inputs may be any that keep to these rules, and one draw needn't show every extreme that they name: `ray_event`: all rays of an event lie on one device; ids count the events of that device. `ray_owner`: within the 128 rays of one device no owner is named more than 2 times, a bound that some block reaches; the 4 owners of one ray differ.
All inputs are finite; a program needn't handle non-finite values.
Results may differ from the reference program's by a relative error of at most 0.0023.
Values may be sent and summed in bfloat16 or wider, within the bound.
No kernel may reach another device: no remote copies, remote signals or barrier semaphores. Data moves between devices by JAX's collectives and lax.ppermute only.
A program may use at most 64 MiB of HBM per device.

```python
import math
import jax
import jax.numpy as jnp
import numpy as np
from jax import lax

SHELLS = 128
PX = 8
PY = 16
NB = 4
E_DEV = 16
R_DEV = 128
NPATCH = 32
TILES = 64
SLAB = 16
CELLS = 4096
RAYS = 65536
CAP = 2
N_DEPTH = 8
DEVICES = 512


def draw_ray_event(key, part):
    events = jax.random.randint(key, (RAYS,), 0, E_DEV, dtype=jnp.int32)
    position = jnp.arange(RAYS, dtype=jnp.int32) % R_DEV
    events = jnp.where(position == 0, E_DEV - 1, events)
    events = jnp.where(position == 1, 0, events)
    return events.astype(jnp.int32)


def touch_ends(drawn, own_key, least, top_value):
    place = [jax.random.randint(jax.random.fold_in(own_key, axis), (), 0, length) for axis, length in enumerate(drawn.shape)]
    longest = drawn.shape.index(max(drawn.shape))
    beside = place[:longest] + [(place[longest] + 1) % drawn.shape[longest]] + place[longest + 1:]
    return drawn.at[tuple(place)].set(least).at[tuple(beside)].set(top_value)


def block_levels(own_key, shape, cuts, least, top_value):
    level = 1.0
    for dim, parts in cuts:
        heights = jax.random.uniform(jax.random.fold_in(jax.random.fold_in(own_key, 6), dim), (parts,), jnp.float32, least / len(cuts), top_value / len(cuts))
        level = level * jnp.repeat(jnp.exp(heights), shape[dim] // parts).reshape((-1,) + (1,) * (len(shape) - 1 - dim))
    return level


def deal_out(stream_key, own, number, rows, number_of, top, reach, lean):
    sequence = jax.random.permutation(stream_key, number_of)
    packed, usual = shares(number_of, rows * top, reach, lean, True), shares(number_of, rows * top, reach, lean, False)
    places = jnp.arange(number_of)

    def named(tallies, rotation):
        used = int((tallies > 0).sum())
        fixed = max(1, used // 4)
        shifted = fixed + (places - fixed + rotation * (used - fixed)) % max(1, number_of - fixed)
        return jnp.zeros((number_of,), jnp.int32).at[sequence[jnp.where(places < fixed, places, shifted)]].set(jnp.asarray(tallies, jnp.int32))

    tallies = jnp.where(number % 4 == 0, named(packed, number // 4), named(usual, number - number // 4 - 1))
    mixed = jax.random.permutation(jax.random.fold_in(own, 3), number_of)
    source_of, taker = mixed[0:number_of // 2 * 2:2], mixed[1:number_of // 2 * 2:2]
    slack = jnp.minimum(tallies[source_of] - 1, reach - tallies[taker]) // 2
    slack = jnp.where((source_of == sequence[0]) | (taker == sequence[0]) | (tallies[taker] == 0), 0, jnp.maximum(slack, 0))
    shifted = jax.random.randint(jax.random.fold_in(own, 4), (number_of // 2,), 0, 1 << 20) % (slack + 1)
    tallies = tallies.at[source_of].add(-shifted).at[taker].add(shifted)
    labels = jnp.searchsorted(jnp.cumsum(tallies), jnp.arange(rows * top), side="right").astype(jnp.int32)
    listing = labels.reshape(top, rows).T
    listing = listing[jax.random.permutation(jax.random.fold_in(own, 1), rows)]
    rotation = jax.random.randint(jax.random.fold_in(own, 2), (rows, 1), 0, top)
    return jnp.take_along_axis(listing, (jnp.arange(top)[None, :] + rotation) % top, axis=1)


def shares(number_of, total, limit, slope, full):
    loads = [(1 << 20) // math.isqrt(grade ** slope) + 1 for grade in range(1, number_of + 1)]
    largest = limit if full else min(limit, max(-(-total // number_of), total * loads[0] // sum(loads)))
    least = 1 if total - largest >= number_of - 1 else 0
    holding, spare = [largest] + [least] * (number_of - 1), total - largest - least * (number_of - 1)
    while spare > 0:
        movable = [i for i in range(1, number_of) if holding[i] < largest] or [i for i in range(1, number_of) if holding[i] < limit]
        mass, left = sum([loads[i] for i in movable]), spare
        for i in movable:
            more = min(limit - holding[i], max(1, left * loads[i] // mass), spare)
            holding[i] = holding[i] + more
            spare = spare - more
    return np.array(holding)


def centred(rng, shape, scale, bound, pieces=(), held_as=jnp.bfloat16):
    values = scale * jax.random.normal(rng, shape, jnp.float32)
    if pieces:
        values = values * block_levels(rng, shape, pieces, -0.22, 0.18)
    return jnp.clip(values, -bound, bound).astype(held_as)


def setup_inputs(seed: int = 0) -> dict:
    streams_of = jax.random.split(jax.random.key(seed), 9)
    residual = centred(streams_of[0], (RAYS,), 3.0, 15.0, ((0, 512),), jnp.float32)
    ray_event = draw_ray_event(jax.random.fold_in(streams_of[8], 71), 0)
    ray_owner_keys = jax.random.split(jax.random.fold_in(streams_of[2], 1), RAYS // R_DEV)
    ray_owner_turns = jax.random.permutation(jax.random.fold_in(streams_of[2], 3), RAYS // R_DEV)
    ray_owner = jax.vmap(lambda own, number: deal_out(jax.random.fold_in(streams_of[2], 2), own, number, R_DEV, DEVICES, NB, CAP, 2))(ray_owner_keys, ray_owner_turns).reshape((RAYS, NB))
    ray_patch = touch_ends(jax.random.randint(streams_of[3], (RAYS, NB), 0, NPATCH), jax.random.fold_in(streams_of[3], 1), 0, NPATCH - 1).astype(jnp.int32)
    tube_center = jnp.clip(1.0 * jax.random.uniform(streams_of[4], (2, RAYS, NB), jnp.float32) ** block_levels(streams_of[4], (2, RAYS, NB), ((1, 512),), -0.2, 0.2), 0.0, 1.0)
    tube_tilt = jnp.clip(jax.random.uniform(streams_of[5], (2, RAYS, NB), jnp.float32, -0.5, 0.5) * block_levels(streams_of[5], (2, RAYS, NB), ((1, 512),), -0.4, 0.0), -0.5, 0.5)
    fresnel = jnp.clip(jnp.exp(jax.random.uniform(streams_of[6], (SHELLS,), jnp.float32, math.log(2.0), math.log(16.0))), 2.0, 16.0)
    radial_width = jnp.clip(jnp.exp(jax.random.uniform(streams_of[7], (SHELLS,), jnp.float32, math.log(1.0), math.log(8.0))), 1.0, 8.0)
    return dict(residual=residual, ray_event=ray_event, ray_owner=ray_owner, ray_patch=ray_patch, tube_center=tube_center, tube_tilt=tube_tilt, fresnel=fresnel, radial_width=radial_width)


def doughnut(center_x, center_y, tilt_x, tilt_y, weights, fresnel_rows):
    slab_size = fresnel_rows.shape[1]
    along_x = jnp.arange(PX).astype(jnp.float32)
    along_y = jnp.arange(PY).astype(jnp.float32)
    within = jnp.arange(slab_size).astype(jnp.float32)
    offset_x = along_x[None, :, None, None] - center_x[:, None, None, None] - tilt_x[:, None, None, None] * within[None, None, None, :]
    offset_y = along_y[None, None, :, None] - center_y[:, None, None, None] - tilt_y[:, None, None, None] * within[None, None, None, :]
    scaled = (offset_x * offset_x + offset_y * offset_y) / fresnel_rows[:, None, None, :]
    values = weights[:, None, None, None] * scaled * jnp.exp(-scaled)
    return values.reshape(values.shape[0], -1).astype(jnp.bfloat16)

def smoother(radial_width):
    shells = radial_width.shape[0]
    levels = jnp.arange(shells).astype(jnp.float32)
    level_gap = levels[:, None] - levels[None, :]
    kernel = jnp.exp(-(level_gap * level_gap) / (2.0 * radial_width[:, None] * radial_width[:, None]))
    return (kernel / lax.optimization_barrier(jnp.sum(kernel, axis=1, keepdims=True))).astype(jnp.bfloat16)

def reference(residual, ray_event, ray_owner, ray_patch, tube_center, tube_tilt, fresnel, radial_width):
    events = ray_event.reshape(DEVICES, R_DEV)
    counts = lax.optimization_barrier(jnp.sum((events[:, :, None] == events[:, None, :]).astype(jnp.int32), axis=2)).reshape(-1)
    weights = residual / jnp.sqrt(counts.astype(jnp.float32))
    owners = ray_owner.reshape(-1).astype(jnp.int32)
    targets = owners * NPATCH + ray_patch.reshape(-1).astype(jnp.int32)
    block_weight = jnp.broadcast_to(weights[:, None], (RAYS, NB)).reshape(-1)
    center_x = tube_center[0].reshape(-1) * PX
    center_y = tube_center[1].reshape(-1) * PY
    tilt_x = tube_tilt[0].reshape(-1)
    tilt_y = tube_tilt[1].reshape(-1)
    fresnel_slabs = fresnel.reshape(N_DEPTH, SLAB)
    batch_size = R_DEV * NB

    def add_blocks(grid_sum, device_step):

        def select_rows(array):
            return lax.dynamic_slice_in_dim(array, device_step * batch_size, batch_size)
        rows_fresnel = fresnel_slabs[select_rows(owners) // TILES]
        values = doughnut(select_rows(center_x), select_rows(center_y), select_rows(tilt_x), select_rows(tilt_y), select_rows(block_weight), rows_fresnel)
        grid_sum = grid_sum.at[select_rows(targets)].add(values.astype(jnp.float32))
        return (grid_sum, None)
    grid_sum = jnp.zeros((DEVICES * NPATCH, PX * PY * SLAB), jnp.float32)
    grid_sum, unused = lax.scan(add_blocks, grid_sum, jnp.arange(DEVICES, dtype=jnp.int32))
    volume = grid_sum.reshape(N_DEPTH, TILES, CELLS, SLAB).transpose(1, 2, 0, 3).reshape(TILES * CELLS, SHELLS).astype(jnp.bfloat16)
    smoothed = jnp.dot(volume, smoother(radial_width).T, preferred_element_type=jnp.float32)
    return smoothed.reshape(TILES, CELLS, SHELLS)
```

```python
import jax
import jax.numpy as jnp
from jax import lax
from jax.experimental import pallas as pl
from jax.experimental.pallas import tpu as pltpu
from jax.sharding import PartitionSpec as P

PX = 8
PY = 16
NPATCH = 32
EVENTS = 16
LANES = 128
WORDS = 8
CHUNK = 256
STRIP = 16

f32 = jnp.float32
bf16 = jnp.bfloat16


def iota(shape, dim):
    return lax.broadcasted_iota(jnp.int32, shape, dim)


def pieces(x):
    high = x.astype(bf16).astype(f32)
    rest = x - high
    middle = rest.astype(bf16).astype(f32)
    return high, middle, rest - middle


def pack_kernel(slab_count, tile_count, residual, event, owner, patch, center, tilt, out):
    devices = slab_count * tile_count
    per_ray, rays = owner.shape
    blocks = per_ray * rays
    group = NPATCH // slab_count
    same = iota((EVENTS, rays), 0) == event[...]
    held = jnp.sum(jnp.where(same, 1.0, 0.0), axis=1, keepdims=True)
    counts = jnp.sum(jnp.where(same, held, 0.0), axis=0, keepdims=True)
    weight = residual[...] / jnp.sqrt(counts)

    def row(x):
        return jnp.concatenate([x[b : b + 1, :] for b in range(per_ray)], axis=1)

    owners, patches = owner[...], patch[...]
    dest = row((patches // group) * tile_count + owners % tile_count)
    place = row((patches % group) * slab_count + owners // tile_count)
    words = [
        jnp.concatenate([weight] * per_ray, axis=1),
        row(center[0]) * PX,
        row(center[1]) * PY,
        row(tilt[0]),
        row(tilt[1]),
        (place + 1).astype(f32),
    ]
    which = iota((WORDS, blocks), 0)
    desc = jnp.zeros((WORDS, blocks), f32)
    for k, word in enumerate(words):
        desc = jnp.where(which == k, word, desc)
    hit = iota((devices, blocks), 0) == dest
    onehot = jnp.where(hit, 1.0, 0.0).astype(bf16)
    before = jnp.where(iota((blocks, blocks), 0) < iota((blocks, blocks), 1), 1.0, 0.0).astype(bf16)
    earlier = jnp.dot(onehot, before, preferred_element_type=f32)
    rank = jnp.sum(jnp.where(hit, earlier, 0.0), axis=0, keepdims=True)
    total = jnp.zeros((devices, LANES), f32)
    for piece in pieces(desc):
        slots = jnp.concatenate(
            [jnp.where(rank == float(s), piece, 0.0) for s in range(LANES // WORDS)], axis=0
        )
        total = total + lax.dot_general(
            onehot, slots.astype(bf16), (((1,), (1,)), ((), ())), preferred_element_type=f32
        )
    out[...] = total


def assemble_kernel(slab_count, arrived, fresnel, width, out, desc_ref, inv_ref, vals_ref, acc_ref):
    sources = arrived.shape[0]
    shells = fresnel.shape[1]
    slab = shells // slab_count
    group = NPATCH // slab_count
    tiles = PX * PY * slab // LANES
    halves = tiles // PX
    per_tile = LANES // slab
    got = arrived[...]
    lane = iota((sources, LANES), 1)
    valid = jnp.where((lane % WORDS == 5) & (got > 0.0), 1.0, 0.0).astype(bf16)
    count = lax.dot_general(
        jnp.ones((8, LANES), bf16), valid, (((1,), (1,)), ((), ())), preferred_element_type=f32
    )
    before = jnp.where(
        iota((sources, sources), 0) < iota((sources, sources), 1), 1.0, 0.0
    ).astype(bf16)
    base = jnp.dot(count.astype(bf16), before, preferred_element_type=f32)
    total = jnp.sum(count[0:1, :]).astype(jnp.int32)
    base = base[0:1, :]
    end = base + count[0:1, :]
    parts = [p.astype(bf16) for p in pieces(got)]
    split = jnp.concatenate(parts, axis=1)

    lanes = iota((CHUNK, LANES), 1)
    row8 = iota((slab_count, LANES), 0)
    lane8 = iota((slab_count, LANES), 1)
    rows = jnp.where(lane8 // slab == row8, fresnel[...], 0.0)
    step = LANES // 2
    while step >= slab:
        rows = rows + pltpu.roll(rows, step, 1)
        step //= 2
    inverse = 1.0 / rows
    table = jnp.concatenate(
        [*pieces(inverse), jnp.zeros((LANES - 3 * slab_count, LANES), f32)], axis=0
    ).astype(bf16)

    acc_ref[...] = jnp.zeros(acc_ref.shape, f32)
    strip_lane = iota((STRIP, LANES), 1)
    shell = (strip_lane % slab).astype(f32)
    across = (strip_lane // slab).astype(f32)

    def chunk(c, carry):
        k = (iota((CHUNK, sources), 0) + c * CHUNK).astype(f32)
        mine = (k >= base) & (k < end)
        pick = jnp.where(mine, 1.0, 0.0).astype(bf16)
        picked = jnp.dot(pick, split, preferred_element_type=f32)
        picked = picked[:, :LANES] + picked[:, LANES : 2 * LANES] + picked[:, 2 * LANES :]
        slot = jnp.sum(jnp.where(mine, k - base, 0.0), axis=1, keepdims=True).astype(jnp.int32)
        desc = jnp.where(lanes // WORDS == slot, picked, 0.0)
        shift = LANES // 2
        while shift >= WORDS:
            desc = desc + pltpu.roll(desc, shift, 1)
            shift //= 2
        desc_ref[...] = desc
        place = desc[:, 5:6].astype(jnp.int32) - 1
        slabs = place & (slab_count - 1)
        rows_of = jnp.where(
            (lanes % slab_count == slabs) & (lanes < 3 * slab_count), 1.0, 0.0
        ).astype(bf16)
        inv_ref[...] = jnp.dot(rows_of, table, preferred_element_type=f32)
        select = jnp.where(
            iota((CHUNK, group * slab_count), 1) == place, 1.0, 0.0
        ).astype(bf16)

        def strip(s, carry):
            at = pl.ds(pl.multiple_of(s * STRIP, STRIP), STRIP)
            d = desc_ref[at, :]
            inv = inv_ref[at, :]
            drift_x = d[:, 1:2] + d[:, 3:4] * shell
            drift_y = d[:, 2:3] + d[:, 4:5] * shell
            sides = []
            for h in range(halves):
                y = (across + float(h * per_tile)) - drift_y
                b = y * y * inv
                q = d[:, 0:1] * jnp.exp(-b)
                sides.append((q, b * q))
            for i in range(PX):
                x = float(i) - drift_x
                a = x * x * inv
                e = jnp.exp(-a)
                p = a * e
                for h in range(halves):
                    q, t = sides[h]
                    lo = (i * halves + h) * LANES
                    vals_ref[at, lo : lo + LANES] = (p * q + e * t).astype(bf16)
            return carry

        lax.fori_loop(0, CHUNK // STRIP, strip, 0)
        acc_ref[...] += lax.dot_general(
            select, vals_ref[...], (((0,), (0,)), ((), ())), preferred_element_type=f32
        )
        return carry

    lax.fori_loop(0, (total + CHUNK - 1) // CHUNK, chunk, 0)

    volume = jnp.concatenate(
        [
            acc_ref[q * slab_count : (q + 1) * slab_count, t * LANES : (t + 1) * LANES]
            for q in range(group)
            for t in range(tiles)
        ],
        axis=0,
    )
    cells = volume.shape[0]
    r = iota((cells, LANES), 0)
    g = iota((cells, LANES), 1) // slab
    bit = 1
    while bit < slab_count:
        up = pltpu.roll(pltpu.roll(volume, cells - bit, 0), bit * slab, 1)
        down = pltpu.roll(pltpu.roll(volume, bit, 0), LANES - bit * slab, 1)
        low = (r & bit) == 0
        volume = jnp.where(
            (r & bit) == (g & bit), volume, jnp.where(low, up, down)
        )
        bit *= 2

    gap = (iota((shells, shells), 0) - iota((shells, shells), 1)).astype(f32)
    kernel = jnp.exp(-(gap * gap) / (2.0 * width[...] * width[...]))
    smooth = (kernel / jnp.sum(kernel, axis=0, keepdims=True)).astype(bf16)
    out[...] = jnp.dot(volume.astype(bf16), smooth, preferred_element_type=f32)


def on_device(
    residual, ray_event, ray_owner, ray_patch, tube_center, tube_tilt, fresnel, radial_width
):
    depth_count = lax.axis_size("depth")
    tile_count = lax.axis_size("tile")
    devices = depth_count * tile_count
    group = NPATCH // depth_count
    shells = fresnel.shape[0]
    slab = shells // depth_count
    vmem = pltpu.CompilerParams(vmem_limit_bytes=48 << 20)
    outgoing = pl.pallas_call(
        lambda *refs: pack_kernel(depth_count, tile_count, *refs),
        out_shape=jax.ShapeDtypeStruct((devices, LANES), f32),
        compiler_params=vmem,
        name="pack",
    )(
        residual[None],
        ray_event[None],
        ray_owner.T,
        ray_patch.T,
        tube_center.transpose(0, 2, 1),
        tube_tilt.transpose(0, 2, 1),
    )
    arrived = lax.all_to_all(
        outgoing[:, None, :], ("depth", "tile"), split_axis=0, concat_axis=0, tiled=True
    )
    smoothed = pl.pallas_call(
        lambda *refs: assemble_kernel(depth_count, *refs),
        out_shape=jax.ShapeDtypeStruct((group * PX * PY, shells), f32),
        scratch_shapes=[
            pltpu.VMEM((CHUNK, LANES), f32),
            pltpu.VMEM((CHUNK, LANES), f32),
            pltpu.VMEM((CHUNK, PX * PY * slab), bf16),
            pltpu.VMEM((group * depth_count, PX * PY * slab), f32),
        ],
        compiler_params=vmem,
        name="assemble",
    )(arrived.reshape(devices, LANES), fresnel[None], radial_width[None])
    return smoothed[None]


def solution(mesh):
    return jax.shard_map(
        on_device,
        mesh=mesh,
        in_specs=(
            P(("depth", "tile")),
            P(("depth", "tile")),
            P(("depth", "tile"), None),
            P(("depth", "tile"), None),
            P(None, ("depth", "tile"), None),
            P(None, ("depth", "tile"), None),
            P(),
            P(),
        ),
        out_specs=P("tile", "depth", None),
        check_vma=False,
    )
```

```python
import jax
import jax.numpy as jnp
from jax import lax
from jax.experimental import pallas as pl
from jax.experimental.pallas import tpu as pltpu
from jax.sharding import PartitionSpec as P

PX = 8
PY = 16
NPATCH = 32
EVENTS = 16
LANES = 128
WORDS = 8
CHUNK = 256
STRIP = 16
UNROLL = 16
LOG2E = 1.4426950408889634
LN2 = 0.6931471805599453

f32 = jnp.float32
bf16 = jnp.bfloat16


def iota(shape, dim):
    return lax.broadcasted_iota(jnp.int32, shape, dim)


def pieces(x):
    high = x.astype(bf16).astype(f32)
    rest = x - high
    middle = rest.astype(bf16).astype(f32)
    return high, middle, rest - middle


def load(pairs, sems):
    copies = [pltpu.make_async_copy(src, dst, sems.at[k]) for k, (src, dst) in enumerate(pairs)]
    for copy in copies:
        copy.start()
    return copies


def pack_kernel(slab_count, tile_count, *refs):
    sources, out, targets, sems = refs[:6], refs[6], refs[7:13], refs[13]
    copies = load(zip(sources, targets), sems)
    residual, event, owner, patch, center, tilt = targets
    devices = slab_count * tile_count
    per_ray, rays = owner.shape
    blocks = per_ray * rays
    group = NPATCH // slab_count
    before = jnp.where(iota((blocks, blocks), 0) < iota((blocks, blocks), 1), 1.0, 0.0).astype(bf16)
    for copy in copies:
        copy.wait()
    same = iota((EVENTS, rays), 0) == event[...]
    held = jnp.sum(jnp.where(same, 1.0, 0.0), axis=1, keepdims=True)
    counts = jnp.sum(jnp.where(same, held, 0.0), axis=0, keepdims=True)
    weight = residual[...] / jnp.sqrt(counts)

    def row(x):
        return jnp.concatenate([x[b : b + 1, :] for b in range(per_ray)], axis=1)

    owners, patches = owner[...], patch[...]
    dest = row((patches // group) * tile_count + owners % tile_count)
    place = row((patches % group) * slab_count + owners // tile_count)
    words = [
        jnp.concatenate([weight] * per_ray, axis=1),
        row(center[0]) * PX,
        row(center[1]) * PY,
        row(tilt[0]),
        row(tilt[1]),
        (place + 1).astype(f32),
    ]
    which = iota((WORDS, blocks), 0)
    desc = jnp.zeros((WORDS, blocks), f32)
    for k, word in enumerate(words):
        desc = jnp.where(which == k, word, desc)
    hit = iota((devices, blocks), 0) == dest
    onehot = jnp.where(hit, 1.0, 0.0).astype(bf16)
    earlier = jnp.dot(onehot, before, preferred_element_type=f32)
    rank = jnp.sum(jnp.where(hit, earlier, 0.0), axis=0, keepdims=True)
    total = jnp.zeros((devices, LANES), f32)
    for piece in pieces(desc):
        slots = jnp.concatenate(
            [jnp.where(rank == float(s), piece, 0.0) for s in range(LANES // WORDS)], axis=0
        )
        total = total + lax.dot_general(
            onehot, slots.astype(bf16), (((1,), (1,)), ((), ())), preferred_element_type=f32
        )
    out[...] = total


def assemble_kernel(slab_count, arrived, fresnel_in, width_in, out, *scratch):
    fresnel, width, desc_ref, inv_ref, vals_ref, acc_ref, result, sems, out_sems = scratch
    copies = load([(fresnel_in, fresnel), (width_in, width)], sems)
    sources = arrived.shape[0]
    shells = fresnel.shape[1]
    slab = shells // slab_count
    slab_bits = slab.bit_length() - 1
    word_bits = WORDS.bit_length() - 1
    group = NPATCH // slab_count
    tiles = PX * PY * slab // LANES
    halves = tiles // PX
    per_tile = LANES // slab
    got = arrived[...]
    lane = iota((sources, LANES), 1)
    valid = jnp.where(((lane & (WORDS - 1)) == 5) & (got > 0.0), 1.0, 0.0).astype(bf16)
    count = lax.dot_general(
        jnp.ones((8, LANES), bf16), valid, (((1,), (1,)), ((), ())), preferred_element_type=f32
    )
    before = jnp.where(
        iota((sources, sources), 0) < iota((sources, sources), 1), 1.0, 0.0
    ).astype(bf16)
    base = jnp.dot(count.astype(bf16), before, preferred_element_type=f32)
    total = jnp.sum(count[0:1, :]).astype(jnp.int32)
    base = base[0:1, :]
    end = base + count[0:1, :]
    split = jnp.concatenate([p.astype(bf16) for p in pieces(got)], axis=1)
    acc_ref[...] = jnp.zeros(acc_ref.shape, f32)

    for copy in copies:
        copy.wait()
    gap = (iota((shells, shells), 0) - iota((shells, shells), 1)).astype(f32)
    kernel = jnp.exp(-(gap * gap) / (2.0 * width[...] * width[...]))
    smooth = (kernel / jnp.sum(kernel, axis=0, keepdims=True)).astype(bf16)
    rows = jnp.where(
        (iota((slab_count, LANES), 1) >> slab_bits) == iota((slab_count, LANES), 0), fresnel[...], 0.0
    )
    step = LANES // 2
    while step >= slab:
        rows = rows + pltpu.roll(rows, step, 1)
        step //= 2
    inverse = -LOG2E / rows
    table = jnp.concatenate(
        [*pieces(inverse), jnp.zeros((LANES - 3 * slab_count, LANES), f32)], axis=0
    ).astype(bf16)

    lanes = iota((CHUNK, LANES), 1)
    slot_of = lanes >> word_bits
    slab_of = jnp.where(lanes < 3 * slab_count, lanes & (slab_count - 1), -1)
    strip_lane = iota((STRIP, LANES), 1)
    shell = (strip_lane & (slab - 1)).astype(f32)
    across = (strip_lane >> slab_bits).astype(f32)
    first = iota((CHUNK, sources), 0).astype(f32)

    def chunk(c, carry):
        done = (c * CHUNK).astype(f32)
        low = base - done
        mine = (first >= low) & (first < end - done)
        pick = jnp.where(mine, 1.0, 0.0).astype(bf16)
        picked = jnp.dot(pick, split, preferred_element_type=f32)
        picked = picked[:, :LANES] + picked[:, LANES : 2 * LANES] + picked[:, 2 * LANES :]
        slot = jnp.sum(jnp.where(mine, first - low, 0.0), axis=1, keepdims=True).astype(jnp.int32)
        desc = jnp.where(slot_of == slot, picked, 0.0)
        shift = LANES // 2
        while shift >= WORDS:
            desc = desc + pltpu.roll(desc, shift, 1)
            shift //= 2
        desc_ref[...] = desc
        place = desc[:, 5:6].astype(jnp.int32) - 1
        rows_of = jnp.where(slab_of == (place & (slab_count - 1)), 1.0, 0.0).astype(bf16)
        inv_ref[...] = jnp.dot(rows_of, table, preferred_element_type=f32)
        select = jnp.where(iota((CHUNK, group * slab_count), 1) == place, 1.0, 0.0).astype(bf16)

        def strip(s, carry):
            at = pl.ds(pl.multiple_of(s * STRIP, STRIP), STRIP)
            d = desc_ref[at, :]
            inv = inv_ref[at, :]
            drift_x = d[:, 1:2] + d[:, 3:4] * shell
            drift_y = d[:, 2:3] + d[:, 4:5] * shell
            weight = d[:, 0:1] * -LN2
            sides = []
            for h in range(halves):
                y = (across + float(h * per_tile)) - drift_y
                b = y * y * inv
                q = weight * jnp.exp2(b)
                sides.append((q, b * q))
            for i in range(PX):
                x = float(i) - drift_x
                a = x * x * inv
                e = jnp.exp2(a)
                p = a * e
                for h in range(halves):
                    q, t = sides[h]
                    lo = (i * halves + h) * LANES
                    vals_ref[at, lo : lo + LANES] = (p * q + e * t).astype(bf16)
            return carry

        lax.fori_loop(0, CHUNK // STRIP, strip, 0, unroll=UNROLL)
        acc_ref[...] += lax.dot_general(
            select, vals_ref[...], (((0,), (0,)), ((), ())), preferred_element_type=f32
        )
        return carry

    lax.fori_loop(0, (total + CHUNK - 1) // CHUNK, chunk, 0)

    shape = (tiles, slab_count, LANES)
    r = iota(shape, 1)
    g = iota(shape, 2) >> slab_bits
    cells = tiles * slab_count
    copies = []
    for q in range(group):
        volume = jnp.stack(
            [
                acc_ref[q * slab_count : (q + 1) * slab_count, t * LANES : (t + 1) * LANES]
                for t in range(tiles)
            ]
        )
        bit = 1
        while bit < slab_count:
            stay = (r & bit) == (g & bit)
            up = pltpu.roll(pltpu.roll(volume, slab_count - bit, 1), bit * slab, 2)
            if 2 * bit == slab_count:
                volume = jnp.where(stay, volume, up)
            else:
                down = pltpu.roll(pltpu.roll(volume, bit, 1), LANES - bit * slab, 2)
                volume = jnp.where(stay, volume, jnp.where((r & bit) == 0, up, down))
            bit *= 2
        at = pl.ds(q * cells, cells)
        result[at, :] = jnp.dot(
            volume.reshape(cells, LANES).astype(bf16), smooth, preferred_element_type=f32
        )
        copies += [pltpu.make_async_copy(result.at[at, :], out.at[at, :], out_sems.at[q])]
        copies[-1].start()
    for copy in copies:
        copy.wait()


def on_device(
    residual, ray_event, ray_owner, ray_patch, tube_center, tube_tilt, fresnel, radial_width
):
    depth_count = lax.axis_size("depth")
    tile_count = lax.axis_size("tile")
    devices = depth_count * tile_count
    group = NPATCH // depth_count
    shells = fresnel.shape[0]
    slab = shells // depth_count
    rays, per_ray = ray_owner.shape
    vmem = pltpu.CompilerParams(vmem_limit_bytes=48 << 20)
    hbm = pl.BlockSpec(memory_space=pltpu.HBM)
    inputs = (
        residual[None],
        ray_event[None],
        ray_owner.T,
        ray_patch.T,
        tube_center.transpose(0, 2, 1),
        tube_tilt.transpose(0, 2, 1),
    )
    inputs = tuple(pltpu.with_memory_space_constraint(x, pltpu.HBM) for x in inputs)
    radial = [pltpu.with_memory_space_constraint(x[None], pltpu.HBM) for x in (fresnel, radial_width)]
    outgoing = pl.pallas_call(
        lambda *refs: pack_kernel(depth_count, tile_count, *refs),
        out_shape=jax.ShapeDtypeStruct((devices, LANES), f32),
        in_specs=[hbm] * len(inputs),
        scratch_shapes=[pltpu.VMEM(x.shape, x.dtype) for x in inputs]
        + [pltpu.SemaphoreType.DMA((len(inputs),))],
        compiler_params=vmem,
        name="pack",
    )(*inputs)
    arrived = lax.all_to_all(
        outgoing[:, None, :], ("depth", "tile"), split_axis=0, concat_axis=0, tiled=True
    )
    cells = group * PX * PY
    smoothed = pl.pallas_call(
        lambda *refs: assemble_kernel(depth_count, *refs),
        out_shape=jax.ShapeDtypeStruct((cells, shells), f32),
        in_specs=[pl.BlockSpec(memory_space=pltpu.VMEM), hbm, hbm],
        out_specs=hbm,
        scratch_shapes=[
            pltpu.VMEM((1, shells), f32),
            pltpu.VMEM((1, shells), f32),
            pltpu.VMEM((CHUNK, LANES), f32),
            pltpu.VMEM((CHUNK, LANES), f32),
            pltpu.VMEM((CHUNK, PX * PY * slab), bf16),
            pltpu.VMEM((group * depth_count, PX * PY * slab), f32),
            pltpu.VMEM((cells, shells), f32),
            pltpu.SemaphoreType.DMA((2,)),
            pltpu.SemaphoreType.DMA((group,)),
        ],
        compiler_params=vmem,
        name="assemble",
    )(arrived.reshape(devices, LANES), *radial)
    return smoothed[None]


def solution(mesh):
    return jax.shard_map(
        on_device,
        mesh=mesh,
        in_specs=(
            P(("depth", "tile")),
            P(("depth", "tile")),
            P(("depth", "tile"), None),
            P(("depth", "tile"), None),
            P(None, ("depth", "tile"), None),
            P(None, ("depth", "tile"), None),
            P(),
            P(),
        ),
        out_specs=P("tile", "depth", None),
        check_vma=False,
    )
```

```python
import jax
import jax.numpy as jnp
from jax import lax
from jax.experimental import pallas as pl
from jax.experimental.pallas import tpu as pltpu
from jax.sharding import PartitionSpec as P

PX = 8
PY = 16
NPATCH = 32
EVENTS = 16
LANES = 128
WORDS = 8
CHUNK = 704
PIECES = 2

f32 = jnp.float32
bf16 = jnp.bfloat16


def iota(shape, dim):
    return lax.broadcasted_iota(jnp.int32, shape, dim)


def pieces(x):
    found = []
    for _ in range(PIECES):
        found.append(x.astype(bf16).astype(f32))
        x = x - found[-1]
    return found


def load(pairs, sems):
    copies = [pltpu.make_async_copy(src, dst, sems.at[k]) for k, (src, dst) in enumerate(pairs)]
    for copy in copies:
        copy.start()
    return copies


def pack_kernel(slab_count, tile_count, *refs):
    sources, out, targets, sems = refs[:6], refs[6], refs[7:13], refs[13]
    copies = load(zip(sources, targets), sems)
    residual, event, owner, patch, center, tilt = targets
    devices = slab_count * tile_count
    per_ray, rays = owner.shape
    blocks = per_ray * rays
    group = NPATCH // slab_count
    before = jnp.where(iota((blocks, blocks), 0) < iota((blocks, blocks), 1), 1.0, 0.0).astype(bf16)
    for copy in copies:
        copy.wait()
    same = iota((EVENTS, rays), 0) == event[...]
    held = jnp.sum(jnp.where(same, 1.0, 0.0), axis=1, keepdims=True)
    counts = jnp.sum(jnp.where(same, held, 0.0), axis=0, keepdims=True)
    weight = residual[...] / jnp.sqrt(counts)

    def row(x):
        return jnp.concatenate([x[b : b + 1, :] for b in range(per_ray)], axis=1)

    owners, patches = owner[...], patch[...]
    dest = row((patches // group) * tile_count + owners % tile_count)
    place = row((patches % group) * slab_count + owners // tile_count)
    words = [
        jnp.concatenate([weight] * per_ray, axis=1),
        row(center[0]) * PX,
        row(center[1]) * PY,
        row(tilt[0]),
        row(tilt[1]),
        (place + 1).astype(f32),
    ]
    which = iota((WORDS, blocks), 0)
    desc = jnp.zeros((WORDS, blocks), f32)
    for k, word in enumerate(words):
        desc = jnp.where(which == k, word, desc)
    hit = iota((devices, blocks), 0) == dest
    onehot = jnp.where(hit, 1.0, 0.0).astype(bf16)
    earlier = jnp.dot(onehot, before, preferred_element_type=f32)
    rank = jnp.sum(jnp.where(hit, earlier, 0.0), axis=0, keepdims=True)
    total = jnp.zeros((devices, LANES), f32)
    for piece in pieces(desc):
        slots = jnp.concatenate(
            [jnp.where(rank == float(s), piece, 0.0) for s in range(LANES // WORDS)], axis=0
        )
        total = total + lax.dot_general(
            onehot, slots.astype(bf16), (((1,), (1,)), ((), ())), preferred_element_type=f32
        )
    out[...] = total


def assemble_kernel(slab_count, arrived, fresnel_in, width_in, out, *scratch):
    fresnel, width, acc_ref, result, sems, out_sems = scratch
    copies = load([(fresnel_in, fresnel), (width_in, width)], sems)
    sources = arrived.shape[0]
    shells = fresnel.shape[1]
    slab = shells // slab_count
    slab_bits = slab.bit_length() - 1
    word_bits = WORDS.bit_length() - 1
    group = NPATCH // slab_count
    tiles = PX * PY * slab // LANES
    halves = tiles // PX
    per_tile = LANES // slab
    got = arrived[...]
    lane = iota((sources, LANES), 1)
    valid = jnp.where(((lane & (WORDS - 1)) == 5) & (got > 0.0), 1.0, 0.0).astype(bf16)
    row_source, column_source = iota((sources, sources), 0), iota((sources, sources), 1)
    count = lax.dot_general(
        jnp.ones((8, LANES), bf16), valid, (((1,), (1,)), ((), ())), preferred_element_type=f32
    )
    before = jnp.where(row_source < column_source, 1.0, 0.0).astype(bf16)
    base = jnp.dot(count.astype(bf16), before, preferred_element_type=f32)
    total = jnp.sum(count[0:1, :]).astype(jnp.int32)
    base = base[0:1, :]
    end = base + count[0:1, :]
    count_down = jnp.dot(valid, jnp.ones((LANES, LANES), bf16), preferred_element_type=f32)
    after = jnp.where(row_source > column_source, 1.0, 0.0).astype(bf16)
    base_down = jnp.dot(after, count_down.astype(bf16), preferred_element_type=f32)
    base_down = (base_down.astype(jnp.int32) & 255).astype(f32).astype(bf16)
    split = jnp.concatenate([*[p.astype(bf16) for p in pieces(got)], base_down], axis=1)
    acc_ref[...] = jnp.zeros(acc_ref.shape, f32)

    for copy in copies:
        copy.wait()
    gap = (iota((shells, shells), 0) - iota((shells, shells), 1)).astype(f32)
    kernel = jnp.exp(-(gap * gap) / (2.0 * width[...] * width[...]))
    smooth = (kernel / jnp.sum(kernel, axis=0, keepdims=True)).astype(bf16)
    small = (slab_count, LANES)
    lane_group = iota(small, 1) >> slab_bits
    rows = jnp.where(lane_group == iota(small, 0), fresnel[...], 0.0)
    step = LANES // 2
    while step >= slab:
        rows = rows + pltpu.roll(rows, step, 1)
        step //= 2
    inverse = -1.0 / rows
    turned = ((iota(small, 0) - lane_group) & (per_tile - 1)).astype(f32)
    rest = jnp.zeros((LANES - PIECES * slab_count, LANES), f32)
    table = jnp.concatenate(
        [
            jnp.concatenate([*pieces(inverse), rest], axis=0),
            jnp.concatenate([turned, jnp.zeros((LANES - slab_count, LANES), f32)], axis=0),
        ],
        axis=1,
    ).astype(bf16)

    slot_of = iota((CHUNK, LANES), 1) >> word_bits
    lanes = iota((CHUNK, LANES), 1)
    slab_of = jnp.where(lanes < PIECES * slab_count, lanes & (slab_count - 1), -1)
    spread = (PIECES * LANES, LANES)
    word = iota(spread, 0) & (WORDS - 1)
    level = (iota(spread, 1) & (slab - 1)).astype(f32)
    spread = jnp.concatenate(
        [
            jnp.where(word == 1, 1.0, jnp.where(word == 3, level, 0.0)),
            jnp.where(word == 2, 1.0, jnp.where(word == 4, level, 0.0)),
            jnp.where(word == 0, -1.0, 0.0),
            jnp.where(word == 5, 1.0, 0.0),
        ],
        axis=1,
    ).astype(bf16)
    one_lane = jnp.where(iota((8, LANES), 1) == 0, 1.0, 0.0).astype(bf16)
    first = iota((CHUNK, sources), 0).astype(f32)

    def chunk(c, carry):
        start = c * CHUNK
        done = start.astype(f32)
        mine = (first >= base - done) & (first < end - done)
        pick = jnp.where(mine, 1.0, 0.0).astype(bf16)
        picked = jnp.dot(pick, split, preferred_element_type=f32)
        slot = (iota((CHUNK, LANES), 0) + start - picked[:, PIECES * LANES :].astype(jnp.int32)) & 255
        here = slot_of == slot
        desc = jnp.concatenate(
            [
                jnp.where(here, picked[:, k * LANES : (k + 1) * LANES], 0.0).astype(bf16)
                for k in range(PIECES)
            ],
            axis=1,
        )
        desc = jnp.dot(desc, spread, preferred_element_type=f32)
        place = desc[:, 3 * LANES :]
        rows_of = jnp.where(slab_of == ((place.astype(jnp.int32) - 1) & (slab_count - 1)), 1.0, 0.0)
        by_slab = jnp.dot(rows_of.astype(bf16), table, preferred_element_type=f32)
        code = lax.dot_general(
            one_lane, place.astype(bf16), (((1,), (1,)), ((), ())), preferred_element_type=f32
        )
        which = iota((group * slab_count, CHUNK), 0).astype(f32) + 1.0
        select = jnp.where(which == code[0:1, :], 1.0, 0.0).astype(bf16)
        inverse = by_slab[:, :LANES]
        drift_x = desc[:, :LANES]
        drift_y = desc[:, LANES : 2 * LANES] - by_slab[:, LANES:]
        weight = desc[:, 2 * LANES : 3 * LANES]
        sides = []
        for h in range(halves):
            y = float(h * per_tile) - drift_y
            b = y * y * inverse
            q = weight * jnp.exp(b)
            sides.append((q, b * q))
        for i in range(PX):
            x = float(i) - drift_x
            a = x * x * inverse
            e = jnp.exp(a)
            values = jnp.concatenate([(e * (a * q + t)).astype(bf16) for q, t in sides], axis=1)
            at = pl.ds(i * halves * LANES, halves * LANES)
            acc_ref[:, at] += jnp.dot(select, values, preferred_element_type=f32)
        return carry

    lax.fori_loop(0, (total + CHUNK - 1) // CHUNK, chunk, 0)

    shape = (tiles, slab_count, LANES)
    g = iota(shape, 2) >> slab_bits
    cells = tiles * slab_count
    copies = []
    for q in range(group):
        volume = jnp.stack(
            [
                acc_ref[q * slab_count : (q + 1) * slab_count, t * LANES : (t + 1) * LANES]
                for t in range(tiles)
            ]
        )
        bit = 1
        while bit < slab_count:
            volume = jnp.where((g & bit) == 0, volume, pltpu.roll(volume, slab_count - bit, 1))
            bit *= 2
        volume = pltpu.roll(volume, 0, 2, stride=slab, stride_axis=1)
        at = pl.ds(q * cells, cells)
        result[at, :] = jnp.dot(
            volume.reshape(cells, LANES).astype(bf16), smooth, preferred_element_type=f32
        )
        copies += [pltpu.make_async_copy(result.at[at, :], out.at[at, :], out_sems.at[q])]
        copies[-1].start()
    for copy in copies:
        copy.wait()


def on_device(
    residual, ray_event, ray_owner, ray_patch, tube_center, tube_tilt, fresnel, radial_width
):
    depth_count = lax.axis_size("depth")
    tile_count = lax.axis_size("tile")
    devices = depth_count * tile_count
    group = NPATCH // depth_count
    shells = fresnel.shape[0]
    slab = shells // depth_count
    rays, per_ray = ray_owner.shape
    vmem = pltpu.CompilerParams(vmem_limit_bytes=48 << 20)
    hbm = pl.BlockSpec(memory_space=pltpu.HBM)
    inputs = (
        residual[None],
        ray_event[None],
        ray_owner.T,
        ray_patch.T,
        tube_center.transpose(0, 2, 1),
        tube_tilt.transpose(0, 2, 1),
    )
    inputs = tuple(pltpu.with_memory_space_constraint(x, pltpu.HBM) for x in inputs)
    radial = [pltpu.with_memory_space_constraint(x[None], pltpu.HBM) for x in (fresnel, radial_width)]
    outgoing = pl.pallas_call(
        lambda *refs: pack_kernel(depth_count, tile_count, *refs),
        out_shape=jax.ShapeDtypeStruct((devices, LANES), f32),
        in_specs=[hbm] * len(inputs),
        scratch_shapes=[pltpu.VMEM(x.shape, x.dtype) for x in inputs]
        + [pltpu.SemaphoreType.DMA((len(inputs),))],
        compiler_params=vmem,
        name="pack",
    )(*inputs)
    arrived = lax.all_to_all(
        outgoing[:, None, :], ("depth", "tile"), split_axis=0, concat_axis=0, tiled=True
    )
    cells = group * PX * PY
    smoothed = pl.pallas_call(
        lambda *refs: assemble_kernel(depth_count, *refs),
        out_shape=jax.ShapeDtypeStruct((cells, shells), f32),
        in_specs=[pl.BlockSpec(memory_space=pltpu.VMEM), hbm, hbm],
        out_specs=hbm,
        scratch_shapes=[
            pltpu.VMEM((1, shells), f32),
            pltpu.VMEM((1, shells), f32),
            pltpu.VMEM((group * depth_count, PX * PY * slab), f32),
            pltpu.VMEM((cells, shells), f32),
            pltpu.SemaphoreType.DMA((2,)),
            pltpu.SemaphoreType.DMA((group,)),
        ],
        compiler_params=vmem,
        name="assemble",
    )(arrived.reshape(devices, LANES), *radial)
    return smoothed[None]


def solution(mesh):
    return jax.shard_map(
        on_device,
        mesh=mesh,
        in_specs=(
            P(("depth", "tile")),
            P(("depth", "tile")),
            P(("depth", "tile"), None),
            P(("depth", "tile"), None),
            P(None, ("depth", "tile"), None),
            P(None, ("depth", "tile"), None),
            P(),
            P(),
        ),
        out_specs=P("tile", "depth", None),
        check_vma=False,
    )
```

```python
import jax
import jax.numpy as jnp
from jax import lax
from jax.experimental import pallas as pl
from jax.experimental.pallas import tpu as pltpu
from jax.sharding import PartitionSpec as P

PX = 8
PY = 16
NPATCH = 32
EVENTS = 16
LANES = 128
WORDS = 8
CHUNK = 768
EXTRA = 128
PIECES = 2

f32 = jnp.float32
bf16 = jnp.bfloat16


def iota(shape, dim):
    return lax.broadcasted_iota(jnp.int32, shape, dim)


def pieces(x):
    found = []
    for _ in range(PIECES):
        found.append(x.astype(bf16).astype(f32))
        x = x - found[-1]
    return found


def load(pairs, sems):
    copies = [pltpu.make_async_copy(src, dst, sems.at[k]) for k, (src, dst) in enumerate(pairs)]
    for copy in copies:
        copy.start()
    return copies


def pack_kernel(slab_count, tile_count, *refs):
    sources, out, targets, sems = refs[:6], refs[6], refs[7:13], refs[13]
    copies = load(zip(sources, targets), sems)
    residual, event, owner, patch, center, tilt = targets
    devices = slab_count * tile_count
    per_ray, rays = owner.shape
    blocks = per_ray * rays
    group = NPATCH // slab_count
    before = jnp.where(iota((blocks, blocks), 0) < iota((blocks, blocks), 1), 1.0, 0.0).astype(bf16)
    for copy in copies:
        copy.wait()
    same = iota((EVENTS, rays), 0) == event[...]
    held = jnp.sum(jnp.where(same, 1.0, 0.0), axis=1, keepdims=True)
    counts = jnp.sum(jnp.where(same, held, 0.0), axis=0, keepdims=True)
    weight = residual[...] / jnp.sqrt(counts)

    def row(x):
        return jnp.concatenate([x[b : b + 1, :] for b in range(per_ray)], axis=1)

    owners, patches = owner[...], patch[...]
    dest = row((patches // group) * tile_count + owners % tile_count)
    place = row((patches % group) * slab_count + owners // tile_count)
    words = [
        jnp.concatenate([weight] * per_ray, axis=1),
        row(center[0]) * PX,
        row(center[1]) * PY,
        row(tilt[0]),
        row(tilt[1]),
        (place + 1).astype(f32),
    ]
    which = iota((WORDS, blocks), 0)
    desc = jnp.zeros((WORDS, blocks), f32)
    for k, word in enumerate(words):
        desc = jnp.where(which == k, word, desc)
    hit = iota((devices, blocks), 0) == dest
    onehot = jnp.where(hit, 1.0, 0.0).astype(bf16)
    earlier = jnp.dot(onehot, before, preferred_element_type=f32)
    rank = jnp.sum(jnp.where(hit, earlier, 0.0), axis=0, keepdims=True)
    slots = jnp.concatenate(
        [
            jnp.where(rank == float(s), piece, 0.0)
            for piece in pieces(desc)
            for s in range(LANES // WORDS)
        ],
        axis=0,
    )
    found = lax.dot_general(
        onehot, slots.astype(bf16), (((1,), (1,)), ((), ())), preferred_element_type=f32
    )
    out[...] = sum(found[:, k * LANES : (k + 1) * LANES] for k in range(PIECES))


def assemble_kernel(slab_count, arrived, fresnel_in, width_in, out, *scratch):
    fresnel, width, acc_ref, result, sems, out_sems = scratch
    copies = load([(fresnel_in, fresnel), (width_in, width)], sems)
    sources = arrived.shape[0]
    shells = fresnel.shape[1]
    slab = shells // slab_count
    slab_bits = slab.bit_length() - 1
    word_bits = WORDS.bit_length() - 1
    group = NPATCH // slab_count
    halves = PY * slab // LANES
    per_tile = LANES // slab
    got = arrived[...]
    lane = iota((sources, LANES), 1)
    valid = jnp.where(((lane & (WORDS - 1)) == 5) & (got > 0.0), 1.0, 0.0).astype(bf16)
    row_source, column_source = iota((sources, sources), 0), iota((sources, sources), 1)
    count = lax.dot_general(
        jnp.ones((8, LANES), bf16), valid, (((1,), (1,)), ((), ())), preferred_element_type=f32
    )
    before = jnp.where(row_source < column_source, 1.0, 0.0).astype(bf16)
    base = jnp.dot(count.astype(bf16), before, preferred_element_type=f32)
    total = jnp.sum(count[0:1, :]).astype(jnp.int32)
    base = base[0:1, :]
    end = base + count[0:1, :]
    count_down = jnp.dot(valid, jnp.ones((LANES, LANES), bf16), preferred_element_type=f32)
    after = jnp.where(row_source > column_source, 1.0, 0.0).astype(bf16)
    base_down = jnp.dot(after, count_down.astype(bf16), preferred_element_type=f32)
    base_down = (base_down.astype(jnp.int32) & 255).astype(f32).astype(bf16)
    split = jnp.concatenate([*[p.astype(bf16) for p in pieces(got)], base_down], axis=1)

    for copy in copies:
        copy.wait()
    gap = (iota((shells, shells), 0) - iota((shells, shells), 1)).astype(f32)
    kernel = jnp.exp(-(gap * gap) / (2.0 * width[...] * width[...]))
    smooth = (kernel / jnp.sum(kernel, axis=0, keepdims=True)).astype(bf16)
    small = (slab_count, LANES)
    lane_group = iota(small, 1) >> slab_bits
    rows = jnp.where(lane_group == iota(small, 0), fresnel[...], 0.0)
    step = LANES // 2
    while step >= slab:
        rows = rows + pltpu.roll(rows, step, 1)
        step //= 2
    inverse = -1.0 / rows
    turned = ((iota(small, 0) - lane_group) & (per_tile - 1)).astype(f32)
    rest = jnp.zeros((LANES - PIECES * slab_count, LANES), f32)
    table = jnp.concatenate(
        [
            jnp.concatenate([*pieces(inverse), rest], axis=0),
            jnp.concatenate([turned, jnp.zeros((LANES - slab_count, LANES), f32)], axis=0),
        ],
        axis=1,
    ).astype(bf16)

    spread = (PIECES * LANES, LANES)
    word = iota(spread, 0) & (WORDS - 1)
    level = (iota(spread, 1) & (slab - 1)).astype(f32)
    spread = jnp.concatenate(
        [
            jnp.where(word == 1, 1.0, jnp.where(word == 3, level, 0.0)),
            jnp.where(word == 2, 1.0, jnp.where(word == 4, level, 0.0)),
            jnp.where(word == 0, -1.0, 0.0),
            jnp.where(word == 5, 1.0, 0.0),
        ],
        axis=1,
    ).astype(bf16)
    one_lane = jnp.where(iota((8, LANES), 1) == 0, 1.0, 0.0).astype(bf16)

    def select_blocks(start, size):
        first = (iota((size, sources), 0) + start).astype(f32)
        mine = (first >= base) & (first < end)
        pick = jnp.where(mine, 1.0, 0.0).astype(bf16)
        picked = jnp.dot(pick, split, preferred_element_type=f32)
        lanes = iota((size, LANES), 1)
        slot = (iota((size, LANES), 0) + start - picked[:, PIECES * LANES :].astype(jnp.int32)) & 255
        here = (lanes >> word_bits) == slot
        desc = jnp.concatenate(
            [
                jnp.where(here, picked[:, k * LANES : (k + 1) * LANES], 0.0).astype(bf16)
                for k in range(PIECES)
            ],
            axis=1,
        )
        desc = jnp.dot(desc, spread, preferred_element_type=f32)
        place = desc[:, 3 * LANES :]
        slab_of = jnp.where(lanes < PIECES * slab_count, lanes & (slab_count - 1), -1)
        rows_of = jnp.where(slab_of == ((place.astype(jnp.int32) - 1) & (slab_count - 1)), 1.0, 0.0)
        by_slab = jnp.dot(rows_of.astype(bf16), table, preferred_element_type=f32)
        code = lax.dot_general(
            one_lane, place.astype(bf16), (((1,), (1,)), ((), ())), preferred_element_type=f32
        )
        which = iota((group * slab_count, size), 0).astype(f32) + 1.0
        select = jnp.where(which == code[0:1, :], 1.0, 0.0).astype(bf16)
        inverse = by_slab[:, :LANES]
        drift_x = desc[:, :LANES]
        drift_y = desc[:, LANES : 2 * LANES] - by_slab[:, LANES:]
        weight = desc[:, 2 * LANES : 3 * LANES]
        sides = []
        for h in range(halves):
            y = float(h * per_tile) - drift_y
            b = y * y * inverse
            q = weight * jnp.exp(b)
            sides.append((q, b * q))

        def column(i):
            x = float(i) - drift_x
            a = x * x * inverse
            e = jnp.exp(a)
            values = jnp.concatenate([(e * (a * q + t)).astype(bf16) for q, t in sides], axis=1)
            return jnp.dot(select, values, preferred_element_type=f32)

        return column

    width_of = halves * LANES

    column = select_blocks(0, CHUNK)
    for i in range(PX):
        acc_ref[:, i * width_of : (i + 1) * width_of] = column(i)

    def more(c, carry):
        column = select_blocks(CHUNK + c * EXTRA, EXTRA)
        for i in range(PX):
            acc_ref[:, i * width_of : (i + 1) * width_of] += column(i)
        return carry

    lax.fori_loop(0, jnp.maximum(total - CHUNK + EXTRA - 1, 0) // EXTRA, more, 0)

    tiles = PX * halves
    cells = tiles * slab_count
    g = iota((tiles, slab_count, LANES), 2) >> slab_bits
    copies = []
    for q in range(group):
        volume = jnp.stack(
            [
                acc_ref[q * slab_count : (q + 1) * slab_count, t * LANES : (t + 1) * LANES]
                for t in range(tiles)
            ]
        )
        bit = 1
        while bit < slab_count:
            volume = jnp.where((g & bit) == 0, volume, pltpu.roll(volume, slab_count - bit, 1))
            bit *= 2
        volume = pltpu.roll(volume, 0, 2, stride=slab, stride_axis=1)
        result[q] = jnp.dot(
            volume.reshape(cells, LANES).astype(bf16), smooth, preferred_element_type=f32
        )
        copies += [pltpu.make_async_copy(result.at[q], out.at[q], out_sems.at[q])]
        copies[-1].start()
    for copy in copies:
        copy.wait()


def on_device(
    residual, ray_event, ray_owner, ray_patch, tube_center, tube_tilt, fresnel, radial_width
):
    depth_count = lax.axis_size("depth")
    tile_count = lax.axis_size("tile")
    devices = depth_count * tile_count
    group = NPATCH // depth_count
    shells = fresnel.shape[0]
    slab = shells // depth_count
    rays, per_ray = ray_owner.shape
    vmem = pltpu.CompilerParams(vmem_limit_bytes=48 << 20)
    hbm = pl.BlockSpec(memory_space=pltpu.HBM)
    inputs = (
        residual[None],
        ray_event[None],
        ray_owner.T,
        ray_patch.T,
        tube_center.transpose(0, 2, 1),
        tube_tilt.transpose(0, 2, 1),
    )
    inputs = tuple(pltpu.with_memory_space_constraint(x, pltpu.HBM) for x in inputs)
    radial = [pltpu.with_memory_space_constraint(x[None], pltpu.HBM) for x in (fresnel, radial_width)]
    outgoing = pl.pallas_call(
        lambda *refs: pack_kernel(depth_count, tile_count, *refs),
        out_shape=jax.ShapeDtypeStruct((devices, LANES), f32),
        in_specs=[hbm] * len(inputs),
        scratch_shapes=[pltpu.VMEM(x.shape, x.dtype) for x in inputs]
        + [pltpu.SemaphoreType.DMA((len(inputs),))],
        compiler_params=vmem,
        name="pack",
    )(*inputs)
    arrived = lax.all_to_all(
        outgoing[:, None, :], ("depth", "tile"), split_axis=0, concat_axis=0, tiled=True
    )
    smoothed = pl.pallas_call(
        lambda *refs: assemble_kernel(depth_count, *refs),
        out_shape=jax.ShapeDtypeStruct((group, PX * PY, shells), f32),
        in_specs=[pl.BlockSpec(memory_space=pltpu.VMEM), hbm, hbm],
        out_specs=hbm,
        scratch_shapes=[
            pltpu.VMEM((1, shells), f32),
            pltpu.VMEM((1, shells), f32),
            pltpu.VMEM((group * depth_count, PX * PY * slab), f32),
            pltpu.VMEM((group, PX * PY, shells), f32),
            pltpu.SemaphoreType.DMA((2,)),
            pltpu.SemaphoreType.DMA((PX,)),
        ],
        compiler_params=vmem,
        name="assemble",
    )(arrived.reshape(devices, LANES), *radial)
    return smoothed.reshape(1, -1, shells)


def solution(mesh):
    return jax.shard_map(
        on_device,
        mesh=mesh,
        in_specs=(
            P(("depth", "tile")),
            P(("depth", "tile")),
            P(("depth", "tile"), None),
            P(("depth", "tile"), None),
            P(None, ("depth", "tile"), None),
            P(None, ("depth", "tile"), None),
            P(),
            P(),
        ),
        out_specs=P("tile", "depth", None),
        check_vma=False,
    )
```

```python
import jax
import jax.numpy as jnp
from jax import lax
from jax.experimental import pallas as pl
from jax.experimental.pallas import tpu as pltpu
from jax.sharding import PartitionSpec as P

PX = 8
PY = 16
NPATCH = 32
EVENTS = 16
LANES = 128
WORDS = 8
CHUNK = 768
EXTRA = 128
SIZES = (512, 640, CHUNK)
PIECES = 2

f32 = jnp.float32
bf16 = jnp.bfloat16


def iota(shape, dim):
    return lax.broadcasted_iota(jnp.int32, shape, dim)


def pieces(x):
    found = []
    for _ in range(PIECES):
        found.append(x.astype(bf16).astype(f32))
        x = x - found[-1]
    return found


def load(pairs, sems):
    copies = [pltpu.make_async_copy(src, dst, sems.at[k]) for k, (src, dst) in enumerate(pairs)]
    for copy in copies:
        copy.start()
    return copies


def pack_kernel(slab_count, tile_count, *refs):
    sources, out, targets, sems = refs[:6], refs[6], refs[7:13], refs[13]
    copies = load(zip(sources, targets), sems)
    residual, event, owner, patch, center, tilt = targets
    devices = slab_count * tile_count
    per_ray, rays = owner.shape
    blocks = per_ray * rays
    group = NPATCH // slab_count
    before = jnp.where(iota((blocks, blocks), 0) < iota((blocks, blocks), 1), 1.0, 0.0).astype(bf16)
    for copy in copies:
        copy.wait()
    same = iota((EVENTS, rays), 0) == event[...]
    held = jnp.sum(jnp.where(same, 1.0, 0.0), axis=1, keepdims=True)
    counts = jnp.sum(jnp.where(same, held, 0.0), axis=0, keepdims=True)
    weight = residual[...] / jnp.sqrt(counts)

    def row(x):
        return jnp.concatenate([x[b : b + 1, :] for b in range(per_ray)], axis=1)

    owners, patches = owner[...], patch[...]
    dest = row((patches // group) * tile_count + owners % tile_count)
    place = row((patches % group) * slab_count + owners // tile_count)
    words = [
        jnp.concatenate([weight] * per_ray, axis=1),
        row(center[0]) * PX,
        row(center[1]) * PY,
        row(tilt[0]),
        row(tilt[1]),
        (place + 1).astype(f32),
    ]
    which = iota((WORDS, blocks), 0)
    desc = jnp.zeros((WORDS, blocks), f32)
    for k, word in enumerate(words):
        desc = jnp.where(which == k, word, desc)
    hit = iota((devices, blocks), 0) == dest
    onehot = jnp.where(hit, 1.0, 0.0).astype(bf16)
    earlier = jnp.dot(onehot, before, preferred_element_type=f32)
    rank = jnp.sum(jnp.where(hit, earlier, 0.0), axis=0, keepdims=True)
    slots = jnp.concatenate(
        [
            jnp.where(rank == float(s), piece, 0.0)
            for piece in pieces(desc)
            for s in range(LANES // WORDS)
        ],
        axis=0,
    )
    found = lax.dot_general(
        onehot, slots.astype(bf16), (((1,), (1,)), ((), ())), preferred_element_type=f32
    )
    out[...] = sum(found[:, k * LANES : (k + 1) * LANES] for k in range(PIECES))


def assemble_kernel(slab_count, arrived, fresnel_in, width_in, out, *scratch):
    fresnel, width, acc_ref, result, sems, out_sems = scratch
    copies = load([(fresnel_in, fresnel), (width_in, width)], sems)
    sources = arrived.shape[0]
    shells = fresnel.shape[1]
    slab = shells // slab_count
    slab_bits = slab.bit_length() - 1
    word_bits = WORDS.bit_length() - 1
    group = NPATCH // slab_count
    halves = PY * slab // LANES
    per_tile = LANES // slab
    got = arrived[...]
    lane = iota((sources, LANES), 1)
    valid = jnp.where(((lane & (WORDS - 1)) == 5) & (got > 0.0), 1.0, 0.0).astype(bf16)
    row_source, column_source = iota((sources, sources), 0), iota((sources, sources), 1)
    count = lax.dot_general(
        jnp.ones((8, LANES), bf16), valid, (((1,), (1,)), ((), ())), preferred_element_type=f32
    )
    before = jnp.where(row_source < column_source, 1.0, 0.0).astype(bf16)
    base = jnp.dot(count.astype(bf16), before, preferred_element_type=f32)
    total = jnp.sum(count[0:1, :]).astype(jnp.int32)
    base = base[0:1, :]
    end = base + count[0:1, :]
    count_down = jnp.dot(valid, jnp.ones((LANES, LANES), bf16), preferred_element_type=f32)
    after = jnp.where(row_source > column_source, 1.0, 0.0).astype(bf16)
    base_down = jnp.dot(after, count_down.astype(bf16), preferred_element_type=f32)
    base_down = (base_down.astype(jnp.int32) & 255).astype(f32).astype(bf16)
    split = jnp.concatenate([*[p.astype(bf16) for p in pieces(got)], base_down], axis=1)

    for copy in copies:
        copy.wait()
    gap = (iota((shells, shells), 0) - iota((shells, shells), 1)).astype(f32)
    kernel = jnp.exp(-(gap * gap) / (2.0 * width[...] * width[...]))
    smooth = (kernel / jnp.sum(kernel, axis=0, keepdims=True)).astype(bf16)
    small = (slab_count, LANES)
    lane_group = iota(small, 1) >> slab_bits
    rows = jnp.where(lane_group == iota(small, 0), fresnel[...], 0.0)
    step = LANES // 2
    while step >= slab:
        rows = rows + pltpu.roll(rows, step, 1)
        step //= 2
    inverse = -1.0 / rows
    turned = ((iota(small, 0) - lane_group) & (per_tile - 1)).astype(f32)
    rest = jnp.zeros((LANES - PIECES * slab_count, LANES), f32)
    table = jnp.concatenate(
        [
            jnp.concatenate([*pieces(inverse), rest], axis=0),
            jnp.concatenate([turned, jnp.zeros((LANES - slab_count, LANES), f32)], axis=0),
        ],
        axis=1,
    ).astype(bf16)

    spread = (PIECES * LANES, LANES)
    word = iota(spread, 0) & (WORDS - 1)
    level = (iota(spread, 1) & (slab - 1)).astype(f32)
    spread = jnp.concatenate(
        [
            jnp.where(word == 1, 1.0, jnp.where(word == 3, level, 0.0)),
            jnp.where(word == 2, 1.0, jnp.where(word == 4, level, 0.0)),
            jnp.where(word == 0, -1.0, 0.0),
            jnp.where(word == 5, 1.0, 0.0),
        ],
        axis=1,
    ).astype(bf16)
    one_lane = jnp.where(iota((8, LANES), 1) == 0, 1.0, 0.0).astype(bf16)

    def select_blocks(start, size):
        first = (iota((size, sources), 0) + start).astype(f32)
        mine = (first >= base) & (first < end)
        pick = jnp.where(mine, 1.0, 0.0).astype(bf16)
        picked = jnp.dot(pick, split, preferred_element_type=f32)
        lanes = iota((size, LANES), 1)
        slot = (iota((size, LANES), 0) + start - picked[:, PIECES * LANES :].astype(jnp.int32)) & 255
        here = (lanes >> word_bits) == slot
        desc = jnp.concatenate(
            [
                jnp.where(here, picked[:, k * LANES : (k + 1) * LANES], 0.0).astype(bf16)
                for k in range(PIECES)
            ],
            axis=1,
        )
        desc = jnp.dot(desc, spread, preferred_element_type=f32)
        place = desc[:, 3 * LANES :]
        slab_of = jnp.where(lanes < PIECES * slab_count, lanes & (slab_count - 1), -1)
        rows_of = jnp.where(slab_of == ((place.astype(jnp.int32) - 1) & (slab_count - 1)), 1.0, 0.0)
        by_slab = jnp.dot(rows_of.astype(bf16), table, preferred_element_type=f32)
        code = lax.dot_general(
            one_lane, place.astype(bf16), (((1,), (1,)), ((), ())), preferred_element_type=f32
        )
        which = iota((group * slab_count, size), 0).astype(f32) + 1.0
        select = jnp.where(which == code[0:1, :], 1.0, 0.0).astype(bf16)
        inverse = by_slab[:, :LANES]
        drift_x = desc[:, :LANES]
        drift_y = desc[:, LANES : 2 * LANES] - by_slab[:, LANES:]
        weight = desc[:, 2 * LANES : 3 * LANES]
        sides = []
        for h in range(halves):
            y = float(h * per_tile) - drift_y
            b = y * y * inverse
            q = weight * jnp.exp(b)
            sides.append((q, b * q))

        def column(i):
            x = float(i) - drift_x
            a = x * x * inverse
            e = jnp.exp(a)
            values = jnp.concatenate([(e * (a * q + t)).astype(bf16) for q, t in sides], axis=1)
            return jnp.dot(select, values, preferred_element_type=f32)

        return column

    width_of = halves * LANES

    def one_pass(size):
        column = select_blocks(0, size)
        for i in range(PX):
            acc_ref[:, i * width_of : (i + 1) * width_of] = column(i)

    for k, size in enumerate(SIZES):
        fits = (total > SIZES[k - 1]) if k else (total >= 0)
        pl.when(fits & (total <= size) if size < CHUNK else fits)(lambda size=size: one_pass(size))

    def more(c, carry):
        column = select_blocks(CHUNK + c * EXTRA, EXTRA)
        for i in range(PX):
            acc_ref[:, i * width_of : (i + 1) * width_of] += column(i)
        return carry

    lax.fori_loop(0, jnp.maximum(total - CHUNK + EXTRA - 1, 0) // EXTRA, more, 0)

    tiles = PX * halves
    cells = tiles * slab_count
    g = iota((tiles, slab_count, LANES), 2) >> slab_bits
    copies = []
    for q in range(group):
        volume = jnp.stack(
            [
                acc_ref[q * slab_count : (q + 1) * slab_count, t * LANES : (t + 1) * LANES]
                for t in range(tiles)
            ]
        )
        bit = 1
        while bit < slab_count:
            volume = jnp.where((g & bit) == 0, volume, pltpu.roll(volume, slab_count - bit, 1))
            bit *= 2
        volume = pltpu.roll(volume, 0, 2, stride=slab, stride_axis=1)
        result[q] = jnp.dot(
            volume.reshape(cells, LANES).astype(bf16), smooth, preferred_element_type=f32
        )
        copies += [pltpu.make_async_copy(result.at[q], out.at[q], out_sems.at[q])]
        copies[-1].start()
    for copy in copies:
        copy.wait()


def on_device(
    residual, ray_event, ray_owner, ray_patch, tube_center, tube_tilt, fresnel, radial_width
):
    depth_count = lax.axis_size("depth")
    tile_count = lax.axis_size("tile")
    devices = depth_count * tile_count
    group = NPATCH // depth_count
    shells = fresnel.shape[0]
    slab = shells // depth_count
    rays, per_ray = ray_owner.shape
    vmem = pltpu.CompilerParams(vmem_limit_bytes=48 << 20)
    hbm = pl.BlockSpec(memory_space=pltpu.HBM)
    inputs = (
        residual[None],
        ray_event[None],
        ray_owner.T,
        ray_patch.T,
        tube_center.transpose(0, 2, 1),
        tube_tilt.transpose(0, 2, 1),
    )
    inputs = tuple(pltpu.with_memory_space_constraint(x, pltpu.HBM) for x in inputs)
    radial = [pltpu.with_memory_space_constraint(x[None], pltpu.HBM) for x in (fresnel, radial_width)]
    outgoing = pl.pallas_call(
        lambda *refs: pack_kernel(depth_count, tile_count, *refs),
        out_shape=jax.ShapeDtypeStruct((devices, LANES), f32),
        in_specs=[hbm] * len(inputs),
        scratch_shapes=[pltpu.VMEM(x.shape, x.dtype) for x in inputs]
        + [pltpu.SemaphoreType.DMA((len(inputs),))],
        compiler_params=vmem,
        name="pack",
    )(*inputs)
    arrived = lax.all_to_all(
        outgoing[:, None, :], ("depth", "tile"), split_axis=0, concat_axis=0, tiled=True
    )
    smoothed = pl.pallas_call(
        lambda *refs: assemble_kernel(depth_count, *refs),
        out_shape=jax.ShapeDtypeStruct((group, PX * PY, shells), f32),
        in_specs=[pl.BlockSpec(memory_space=pltpu.VMEM), hbm, hbm],
        out_specs=hbm,
        scratch_shapes=[
            pltpu.VMEM((1, shells), f32),
            pltpu.VMEM((1, shells), f32),
            pltpu.VMEM((group * depth_count, PX * PY * slab), f32),
            pltpu.VMEM((group, PX * PY, shells), f32),
            pltpu.SemaphoreType.DMA((2,)),
            pltpu.SemaphoreType.DMA((PX,)),
        ],
        compiler_params=vmem,
        name="assemble",
    )(arrived.reshape(devices, LANES), *radial)
    return smoothed.reshape(1, -1, shells)


def solution(mesh):
    return jax.shard_map(
        on_device,
        mesh=mesh,
        in_specs=(
            P(("depth", "tile")),
            P(("depth", "tile")),
            P(("depth", "tile"), None),
            P(("depth", "tile"), None),
            P(None, ("depth", "tile"), None),
            P(None, ("depth", "tile"), None),
            P(),
            P(),
        ),
        out_specs=P("tile", "depth", None),
        check_vma=False,
    )
```

```python
import jax
import jax.numpy as jnp
from jax import lax
from jax.experimental import pallas as pl
from jax.experimental.pallas import tpu as pltpu
from jax.sharding import PartitionSpec as P

PX = 8
PY = 16
NPATCH = 32
EVENTS = 16
LANES = 128
WORDS = 8
CHUNK = 768
EXTRA = 128
SIZES = (512, 640, CHUNK)
PIECES = 2

f32 = jnp.float32
bf16 = jnp.bfloat16


def iota(shape, dim):
    return lax.broadcasted_iota(jnp.int32, shape, dim)


def pieces(x):
    found = []
    for _ in range(PIECES):
        found.append(x.astype(bf16).astype(f32))
        x = x - found[-1]
    return found


def load(pairs, sems):
    copies = [pltpu.make_async_copy(src, dst, sems.at[k]) for k, (src, dst) in enumerate(pairs)]
    for copy in copies:
        copy.start()
    return copies


def pack_kernel(slab_count, tile_count, *refs):
    sources, out, targets, sems = refs[:6], refs[6], refs[7:13], refs[13]
    copies = load(zip(sources, targets), sems)
    residual, event, owner, patch, center, tilt = targets
    devices = slab_count * tile_count
    per_ray, rays = owner.shape
    blocks = per_ray * rays
    group = NPATCH // slab_count
    before = jnp.where(iota((blocks, blocks), 0) < iota((blocks, blocks), 1), 1.0, 0.0).astype(bf16)
    for copy in copies:
        copy.wait()
    same = iota((EVENTS, rays), 0) == event[...]
    held = jnp.sum(jnp.where(same, 1.0, 0.0), axis=1, keepdims=True)
    counts = jnp.sum(jnp.where(same, held, 0.0), axis=0, keepdims=True)
    weight = residual[...] / jnp.sqrt(counts)

    def row(x):
        return jnp.concatenate([x[b : b + 1, :] for b in range(per_ray)], axis=1)

    owners, patches = owner[...], patch[...]
    dest = row((patches // group) * tile_count + owners % tile_count)
    place = row((patches % group) * slab_count + owners // tile_count)
    words = [
        jnp.concatenate([weight] * per_ray, axis=1),
        row(center[0]) * PX,
        row(center[1]) * PY,
        row(tilt[0]),
        row(tilt[1]),
        (place + 1).astype(f32),
    ]
    which = iota((WORDS, blocks), 0)
    desc = jnp.zeros((WORDS, blocks), f32)
    for k, word in enumerate(words):
        desc = jnp.where(which == k, word, desc)
    hit = iota((devices, blocks), 0) == dest
    onehot = jnp.where(hit, 1.0, 0.0).astype(bf16)
    half = blocks // 2
    left, right = onehot[:, :half], onehot[:, half:]
    triangle = before[:half, :half]
    earlier = jnp.concatenate(
        [
            jnp.dot(left, triangle, preferred_element_type=f32),
            jnp.sum(left.astype(f32), axis=1, keepdims=True)
            + jnp.dot(right, triangle, preferred_element_type=f32),
        ],
        axis=1,
    )
    rank = jnp.sum(jnp.where(hit, earlier, 0.0), axis=0, keepdims=True)
    slots = jnp.concatenate(
        [
            jnp.where(rank == float(s), piece, 0.0)
            for piece in pieces(desc)
            for s in range(LANES // WORDS)
        ],
        axis=0,
    )
    found = lax.dot_general(
        onehot, slots.astype(bf16), (((1,), (1,)), ((), ())), preferred_element_type=f32
    )
    out[...] = sum(found[:, k * LANES : (k + 1) * LANES] for k in range(PIECES))


def assemble_kernel(slab_count, arrived, fresnel_in, width_in, out, *scratch):
    fresnel, width, acc_ref, result, sems, out_sems = scratch
    copies = load([(fresnel_in, fresnel), (width_in, width)], sems)
    sources = arrived.shape[0]
    shells = fresnel.shape[1]
    slab = shells // slab_count
    slab_bits = slab.bit_length() - 1
    word_bits = WORDS.bit_length() - 1
    group = NPATCH // slab_count
    halves = PY * slab // LANES
    per_tile = LANES // slab
    got = arrived[...]
    lane = iota((sources, LANES), 1)
    valid = jnp.where(((lane & (WORDS - 1)) == 5) & (got > 0.0), 1.0, 0.0).astype(bf16)
    row_source, column_source = iota((sources, sources), 0), iota((sources, sources), 1)
    count = lax.dot_general(
        jnp.ones((8, LANES), bf16), valid, (((1,), (1,)), ((), ())), preferred_element_type=f32
    )
    before = jnp.where(row_source < column_source, 1.0, 0.0).astype(bf16)
    base = jnp.dot(count.astype(bf16), before, preferred_element_type=f32)
    total = jnp.sum(count[0:1, :]).astype(jnp.int32)
    base = base[0:1, :]
    end = base + count[0:1, :]
    count_down = jnp.dot(valid, jnp.ones((LANES, LANES), bf16), preferred_element_type=f32)
    after = jnp.where(row_source > column_source, 1.0, 0.0).astype(bf16)
    base_down = jnp.dot(after, count_down.astype(bf16), preferred_element_type=f32)
    base_down = (base_down.astype(jnp.int32) & 255).astype(f32).astype(bf16)
    split = jnp.concatenate([*[p.astype(bf16) for p in pieces(got)], base_down], axis=1)

    for copy in copies:
        copy.wait()
    gap = (iota((shells, shells), 0) - iota((shells, shells), 1)).astype(f32)
    kernel = jnp.exp(-(gap * gap) / (2.0 * width[...] * width[...]))
    smooth = (kernel / jnp.sum(kernel, axis=0, keepdims=True)).astype(bf16)
    small = (slab_count, LANES)
    lane_group = iota(small, 1) >> slab_bits
    rows = jnp.where(lane_group == iota(small, 0), fresnel[...], 0.0)
    step = LANES // 2
    while step >= slab:
        rows = rows + pltpu.roll(rows, step, 1)
        step //= 2
    inverse = -1.0 / rows
    turned = ((iota(small, 0) - lane_group) & (per_tile - 1)).astype(f32)
    rest = jnp.zeros((LANES - PIECES * slab_count, LANES), f32)
    table = jnp.concatenate(
        [
            jnp.concatenate([*pieces(inverse), rest], axis=0),
            jnp.concatenate([turned, jnp.zeros((LANES - slab_count, LANES), f32)], axis=0),
        ],
        axis=1,
    ).astype(bf16)

    spread = (PIECES * LANES, LANES)
    word = iota(spread, 0) & (WORDS - 1)
    level = (iota(spread, 1) & (slab - 1)).astype(f32)
    spread = jnp.concatenate(
        [
            jnp.where(word == 1, 1.0, jnp.where(word == 3, level, 0.0)),
            jnp.where(word == 2, 1.0, jnp.where(word == 4, level, 0.0)),
            jnp.where(word == 0, -1.0, 0.0),
            jnp.where(word == 5, 1.0, 0.0),
        ],
        axis=1,
    ).astype(bf16)
    one_lane = jnp.where(iota((8, LANES), 1) == 0, 1.0, 0.0).astype(bf16)

    def select_blocks(start, size):
        first = (iota((size, sources), 0) + start).astype(f32)
        mine = (first >= base) & (first < end)
        pick = jnp.where(mine, 1.0, 0.0).astype(bf16)
        picked = jnp.dot(pick, split, preferred_element_type=f32)
        lanes = iota((size, LANES), 1)
        slot = (iota((size, LANES), 0) + start - picked[:, PIECES * LANES :].astype(jnp.int32)) & 255
        here = (lanes >> word_bits) == slot
        desc = jnp.concatenate(
            [
                jnp.where(here, picked[:, k * LANES : (k + 1) * LANES], 0.0).astype(bf16)
                for k in range(PIECES)
            ],
            axis=1,
        )
        desc = jnp.dot(desc, spread, preferred_element_type=f32)
        place = desc[:, 3 * LANES :]
        slab_of = jnp.where(lanes < PIECES * slab_count, lanes & (slab_count - 1), -1)
        rows_of = jnp.where(slab_of == ((place.astype(jnp.int32) - 1) & (slab_count - 1)), 1.0, 0.0)
        by_slab = jnp.dot(rows_of.astype(bf16), table, preferred_element_type=f32)
        code = lax.dot_general(
            one_lane, place.astype(bf16), (((1,), (1,)), ((), ())), preferred_element_type=f32
        )
        which = iota((group * slab_count, size), 0).astype(f32) + 1.0
        select = jnp.where(which == code[0:1, :], 1.0, 0.0).astype(bf16)
        inverse = by_slab[:, :LANES]
        drift_x = desc[:, :LANES]
        drift_y = desc[:, LANES : 2 * LANES] - by_slab[:, LANES:]
        weight = desc[:, 2 * LANES : 3 * LANES]
        sides = []
        for h in range(halves):
            y = float(h * per_tile) - drift_y
            b = y * y * inverse
            q = weight * jnp.exp(b)
            sides.append((q, b * q))

        def column(i):
            x = float(i) - drift_x
            a = x * x * inverse
            e = jnp.exp(a)
            values = jnp.concatenate([(e * (a * q + t)).astype(bf16) for q, t in sides], axis=1)
            return jnp.dot(select, values, preferred_element_type=f32)

        return column

    width_of = halves * LANES

    def one_pass(size):
        column = select_blocks(0, size)
        for i in range(PX):
            acc_ref[:, i * width_of : (i + 1) * width_of] = column(i)

    for k, size in enumerate(SIZES):
        fits = (total > SIZES[k - 1]) if k else (total >= 0)
        pl.when(fits & (total <= size) if size < CHUNK else fits)(lambda size=size: one_pass(size))

    def more(c, carry):
        column = select_blocks(CHUNK + c * EXTRA, EXTRA)
        for i in range(PX):
            acc_ref[:, i * width_of : (i + 1) * width_of] += column(i)
        return carry

    lax.fori_loop(0, jnp.maximum(total - CHUNK + EXTRA - 1, 0) // EXTRA, more, 0)

    tiles = PX * halves
    cells = tiles * slab_count
    g = iota((tiles, slab_count, LANES), 2) >> slab_bits
    copies = []
    for q in range(group):
        volume = jnp.stack(
            [
                acc_ref[q * slab_count : (q + 1) * slab_count, t * LANES : (t + 1) * LANES]
                for t in range(tiles)
            ]
        )
        bit = 1
        while bit < slab_count:
            volume = jnp.where((g & bit) == 0, volume, pltpu.roll(volume, slab_count - bit, 1))
            bit *= 2
        volume = pltpu.roll(volume, 0, 2, stride=slab, stride_axis=1)
        result[q] = jnp.dot(
            volume.reshape(cells, LANES).astype(bf16), smooth, preferred_element_type=f32
        )
        copies += [pltpu.make_async_copy(result.at[q], out.at[q], out_sems.at[q])]
        copies[-1].start()
    for copy in copies:
        copy.wait()


def on_device(
    residual, ray_event, ray_owner, ray_patch, tube_center, tube_tilt, fresnel, radial_width
):
    depth_count = lax.axis_size("depth")
    tile_count = lax.axis_size("tile")
    devices = depth_count * tile_count
    group = NPATCH // depth_count
    shells = fresnel.shape[0]
    slab = shells // depth_count
    rays, per_ray = ray_owner.shape
    vmem = pltpu.CompilerParams(vmem_limit_bytes=48 << 20)
    hbm = pl.BlockSpec(memory_space=pltpu.HBM)
    inputs = (
        residual[None],
        ray_event[None],
        ray_owner.T,
        ray_patch.T,
        tube_center.transpose(0, 2, 1),
        tube_tilt.transpose(0, 2, 1),
    )
    inputs = tuple(pltpu.with_memory_space_constraint(x, pltpu.HBM) for x in inputs)
    radial = [pltpu.with_memory_space_constraint(x[None], pltpu.HBM) for x in (fresnel, radial_width)]
    outgoing = pl.pallas_call(
        lambda *refs: pack_kernel(depth_count, tile_count, *refs),
        out_shape=jax.ShapeDtypeStruct((devices, LANES), f32),
        in_specs=[hbm] * len(inputs),
        scratch_shapes=[pltpu.VMEM(x.shape, x.dtype) for x in inputs]
        + [pltpu.SemaphoreType.DMA((len(inputs),))],
        compiler_params=vmem,
        name="pack",
    )(*inputs)
    arrived = lax.all_to_all(
        outgoing[:, None, :], ("depth", "tile"), split_axis=0, concat_axis=0, tiled=True
    )
    smoothed = pl.pallas_call(
        lambda *refs: assemble_kernel(depth_count, *refs),
        out_shape=jax.ShapeDtypeStruct((group, PX * PY, shells), f32),
        in_specs=[pl.BlockSpec(memory_space=pltpu.VMEM), hbm, hbm],
        out_specs=hbm,
        scratch_shapes=[
            pltpu.VMEM((1, shells), f32),
            pltpu.VMEM((1, shells), f32),
            pltpu.VMEM((group * depth_count, PX * PY * slab), f32),
            pltpu.VMEM((group, PX * PY, shells), f32),
            pltpu.SemaphoreType.DMA((2,)),
            pltpu.SemaphoreType.DMA((PX,)),
        ],
        compiler_params=vmem,
        name="assemble",
    )(arrived.reshape(devices, LANES), *radial)
    return smoothed.reshape(1, -1, shells)


def solution(mesh):
    return jax.shard_map(
        on_device,
        mesh=mesh,
        in_specs=(
            P(("depth", "tile")),
            P(("depth", "tile")),
            P(("depth", "tile"), None),
            P(("depth", "tile"), None),
            P(None, ("depth", "tile"), None),
            P(None, ("depth", "tile"), None),
            P(),
            P(),
        ),
        out_specs=P("tile", "depth", None),
        check_vma=False,
    )
```

```python
import jax
import jax.numpy as jnp
from jax import lax
from jax.experimental import pallas as pl
from jax.experimental.pallas import tpu as pltpu
from jax.sharding import PartitionSpec as P

PX = 8
PY = 16
NPATCH = 32
EVENTS = 16
LANES = 128
WORDS = 8
CHUNK = 768
EXTRA = 128
SIZES = (512, 640, CHUNK)
PIECES = 2

f32 = jnp.float32
bf16 = jnp.bfloat16


def iota(shape, dim):
    return lax.broadcasted_iota(jnp.int32, shape, dim)


def pieces(x):
    found = []
    for _ in range(PIECES):
        found.append(x.astype(bf16).astype(f32))
        x = x - found[-1]
    return found


def load(pairs, sems):
    copies = [pltpu.make_async_copy(src, dst, sems.at[k]) for k, (src, dst) in enumerate(pairs)]
    for copy in copies:
        copy.start()
    return copies


def pack_kernel(slab_count, tile_count, *refs):
    sources, out, targets, sems = refs[:6], refs[6], refs[7:13], refs[13]
    copies = load(zip(sources, targets), sems)
    residual, event, owner, patch, center, tilt = targets
    devices = slab_count * tile_count
    per_ray, rays = owner.shape
    blocks = per_ray * rays
    group = NPATCH // slab_count
    triangle = jnp.where(iota((rays, rays), 0) < iota((rays, rays), 1), 1.0, 0.0).astype(bf16)
    for copy in copies:
        copy.wait()
    same = iota((EVENTS, rays), 0) == event[...]
    held = jnp.sum(jnp.where(same, 1.0, 0.0), axis=1, keepdims=True)
    counts = jnp.sum(jnp.where(same, held, 0.0), axis=0, keepdims=True)
    weight = residual[...] / jnp.sqrt(counts)

    def row(x):
        return jnp.concatenate([x[b : b + 1, :] for b in range(per_ray)], axis=1)

    owners, patches = owner[...], patch[...]
    dest = row((patches // group) * tile_count + owners % tile_count)
    place = row((patches % group) * slab_count + owners // tile_count)
    words = [
        jnp.concatenate([weight] * per_ray, axis=1),
        row(center[0]) * PX,
        row(center[1]) * PY,
        row(tilt[0]),
        row(tilt[1]),
        (place + 1).astype(f32),
    ]
    which = iota((WORDS, blocks), 0)
    desc = jnp.zeros((WORDS, blocks), f32)
    for k, word in enumerate(words):
        desc = jnp.where(which == k, word, desc)
    hit = iota((devices, blocks), 0) == dest
    onehot = jnp.where(hit, 1.0, 0.0).astype(bf16)
    earlier, so_far = [], 0.0
    for b in range(per_ray):
        part = onehot[:, b * rays : (b + 1) * rays]
        earlier.append(so_far + jnp.dot(part, triangle, preferred_element_type=f32))
        so_far = so_far + jnp.sum(part.astype(f32), axis=1, keepdims=True)
    earlier = jnp.concatenate(earlier, axis=1)
    rank = jnp.sum(jnp.where(hit, earlier, 0.0), axis=0, keepdims=True)
    slots = jnp.concatenate(
        [
            jnp.where(rank == float(s), piece, 0.0)
            for piece in pieces(desc)
            for s in range(LANES // WORDS)
        ],
        axis=0,
    )
    found = lax.dot_general(
        onehot, slots.astype(bf16), (((1,), (1,)), ((), ())), preferred_element_type=f32
    )
    out[...] = sum(found[:, k * LANES : (k + 1) * LANES] for k in range(PIECES))


def assemble_kernel(slab_count, arrived, fresnel_in, width_in, out, *scratch):
    fresnel, width, acc_ref, result, sems, out_sems = scratch
    copies = load([(fresnel_in, fresnel), (width_in, width)], sems)
    sources = arrived.shape[0]
    shells = fresnel.shape[1]
    slab = shells // slab_count
    slab_bits = slab.bit_length() - 1
    word_bits = WORDS.bit_length() - 1
    group = NPATCH // slab_count
    halves = PY * slab // LANES
    per_tile = LANES // slab
    got = arrived[...]
    lane = iota((sources, LANES), 1)
    valid = jnp.where(((lane & (WORDS - 1)) == 5) & (got > 0.0), 1.0, 0.0).astype(bf16)
    row_source, column_source = iota((sources, sources), 0), iota((sources, sources), 1)
    count = lax.dot_general(
        jnp.ones((8, LANES), bf16), valid, (((1,), (1,)), ((), ())), preferred_element_type=f32
    )
    before = jnp.where(row_source < column_source, 1.0, 0.0).astype(bf16)
    base = jnp.dot(count.astype(bf16), before, preferred_element_type=f32)
    total = jnp.sum(count[0:1, :]).astype(jnp.int32)
    base = base[0:1, :]
    end = base + count[0:1, :]
    count_down = jnp.dot(valid, jnp.ones((LANES, LANES), bf16), preferred_element_type=f32)
    after = jnp.where(row_source > column_source, 1.0, 0.0).astype(bf16)
    base_down = jnp.dot(after, count_down.astype(bf16), preferred_element_type=f32)
    base_down = (base_down.astype(jnp.int32) & 255).astype(f32).astype(bf16)
    split = jnp.concatenate([*[p.astype(bf16) for p in pieces(got)], base_down], axis=1)

    for copy in copies:
        copy.wait()
    gap = (iota((shells, shells), 0) - iota((shells, shells), 1)).astype(f32)
    kernel = jnp.exp(-(gap * gap) / (2.0 * width[...] * width[...]))
    smooth = (kernel / jnp.sum(kernel, axis=0, keepdims=True)).astype(bf16)
    small = (slab_count, LANES)
    lane_group = iota(small, 1) >> slab_bits
    rows = jnp.where(lane_group == iota(small, 0), fresnel[...], 0.0)
    step = LANES // 2
    while step >= slab:
        rows = rows + pltpu.roll(rows, step, 1)
        step //= 2
    inverse = -1.0 / rows
    turned = ((iota(small, 0) - lane_group) & (per_tile - 1)).astype(f32)
    rest = jnp.zeros((LANES - PIECES * slab_count, LANES), f32)
    table = jnp.concatenate(
        [
            jnp.concatenate([*pieces(inverse), rest], axis=0),
            jnp.concatenate([turned, jnp.zeros((LANES - slab_count, LANES), f32)], axis=0),
        ],
        axis=1,
    ).astype(bf16)

    spread = (PIECES * LANES, LANES)
    word = iota(spread, 0) & (WORDS - 1)
    level = (iota(spread, 1) & (slab - 1)).astype(f32)
    spread = jnp.concatenate(
        [
            jnp.where(word == 1, 1.0, jnp.where(word == 3, level, 0.0)),
            jnp.where(word == 2, 1.0, jnp.where(word == 4, level, 0.0)),
            jnp.where(word == 0, -1.0, 0.0),
            jnp.where(word == 5, 1.0, 0.0),
        ],
        axis=1,
    ).astype(bf16)
    one_lane = jnp.where(iota((8, LANES), 1) == 0, 1.0, 0.0).astype(bf16)

    def select_blocks(start, size):
        first = (iota((size, sources), 0) + start).astype(f32)
        mine = (first >= base) & (first < end)
        pick = jnp.where(mine, 1.0, 0.0).astype(bf16)
        picked = jnp.dot(pick, split, preferred_element_type=f32)
        lanes = iota((size, LANES), 1)
        slot = (iota((size, LANES), 0) + start - picked[:, PIECES * LANES :].astype(jnp.int32)) & 255
        here = (lanes >> word_bits) == slot
        desc = jnp.concatenate(
            [
                jnp.where(here, picked[:, k * LANES : (k + 1) * LANES], 0.0).astype(bf16)
                for k in range(PIECES)
            ],
            axis=1,
        )
        desc = jnp.dot(desc, spread, preferred_element_type=f32)
        place = desc[:, 3 * LANES :]
        slab_of = jnp.where(lanes < PIECES * slab_count, lanes & (slab_count - 1), -1)
        rows_of = jnp.where(slab_of == ((place.astype(jnp.int32) - 1) & (slab_count - 1)), 1.0, 0.0)
        by_slab = jnp.dot(rows_of.astype(bf16), table, preferred_element_type=f32)
        code = lax.dot_general(
            one_lane, place.astype(bf16), (((1,), (1,)), ((), ())), preferred_element_type=f32
        )
        which = iota((group * slab_count, size), 0).astype(f32) + 1.0
        select = jnp.where(which == code[0:1, :], 1.0, 0.0).astype(bf16)
        inverse = by_slab[:, :LANES]
        drift_x = desc[:, :LANES]
        drift_y = desc[:, LANES : 2 * LANES] - by_slab[:, LANES:]
        weight = desc[:, 2 * LANES : 3 * LANES]
        sides = []
        for h in range(halves):
            y = float(h * per_tile) - drift_y
            b = y * y * inverse
            q = weight * jnp.exp(b)
            sides.append((q, b * q))

        def column(i):
            x = float(i) - drift_x
            a = x * x * inverse
            e = jnp.exp(a)
            values = jnp.concatenate([(e * (a * q + t)).astype(bf16) for q, t in sides], axis=1)
            return jnp.dot(select, values, preferred_element_type=f32)

        return column

    width_of = halves * LANES

    def one_pass(size):
        column = select_blocks(0, size)
        for i in range(PX):
            acc_ref[:, i * width_of : (i + 1) * width_of] = column(i)

    for k, size in enumerate(SIZES):
        fits = (total > SIZES[k - 1]) if k else (total >= 0)
        pl.when(fits & (total <= size) if size < CHUNK else fits)(lambda size=size: one_pass(size))

    def more(c, carry):
        column = select_blocks(CHUNK + c * EXTRA, EXTRA)
        for i in range(PX):
            acc_ref[:, i * width_of : (i + 1) * width_of] += column(i)
        return carry

    lax.fori_loop(0, jnp.maximum(total - CHUNK + EXTRA - 1, 0) // EXTRA, more, 0)

    tiles = PX * halves
    cells = tiles * slab_count
    g = iota((tiles, slab_count, LANES), 2) >> slab_bits
    copies = []
    for q in range(group):
        volume = jnp.stack(
            [
                acc_ref[q * slab_count : (q + 1) * slab_count, t * LANES : (t + 1) * LANES]
                for t in range(tiles)
            ]
        )
        bit = 1
        while bit < slab_count:
            volume = jnp.where((g & bit) == 0, volume, pltpu.roll(volume, slab_count - bit, 1))
            bit *= 2
        volume = pltpu.roll(volume, 0, 2, stride=slab, stride_axis=1)
        result[q] = jnp.dot(
            volume.reshape(cells, LANES).astype(bf16), smooth, preferred_element_type=f32
        )
        copies += [pltpu.make_async_copy(result.at[q], out.at[q], out_sems.at[q])]
        copies[-1].start()
    for copy in copies:
        copy.wait()


def on_device(
    residual, ray_event, ray_owner, ray_patch, tube_center, tube_tilt, fresnel, radial_width
):
    depth_count = lax.axis_size("depth")
    tile_count = lax.axis_size("tile")
    devices = depth_count * tile_count
    group = NPATCH // depth_count
    shells = fresnel.shape[0]
    slab = shells // depth_count
    rays, per_ray = ray_owner.shape
    vmem = pltpu.CompilerParams(vmem_limit_bytes=48 << 20)
    hbm = pl.BlockSpec(memory_space=pltpu.HBM)
    inputs = (
        residual[None],
        ray_event[None],
        ray_owner.T,
        ray_patch.T,
        tube_center.transpose(0, 2, 1),
        tube_tilt.transpose(0, 2, 1),
    )
    inputs = tuple(pltpu.with_memory_space_constraint(x, pltpu.HBM) for x in inputs)
    radial = [pltpu.with_memory_space_constraint(x[None], pltpu.HBM) for x in (fresnel, radial_width)]
    outgoing = pl.pallas_call(
        lambda *refs: pack_kernel(depth_count, tile_count, *refs),
        out_shape=jax.ShapeDtypeStruct((devices, LANES), f32),
        in_specs=[hbm] * len(inputs),
        scratch_shapes=[pltpu.VMEM(x.shape, x.dtype) for x in inputs]
        + [pltpu.SemaphoreType.DMA((len(inputs),))],
        compiler_params=vmem,
        name="pack",
    )(*inputs)
    arrived = lax.all_to_all(
        outgoing[:, None, :], ("depth", "tile"), split_axis=0, concat_axis=0, tiled=True
    )
    smoothed = pl.pallas_call(
        lambda *refs: assemble_kernel(depth_count, *refs),
        out_shape=jax.ShapeDtypeStruct((group, PX * PY, shells), f32),
        in_specs=[pl.BlockSpec(memory_space=pltpu.VMEM), hbm, hbm],
        out_specs=hbm,
        scratch_shapes=[
            pltpu.VMEM((1, shells), f32),
            pltpu.VMEM((1, shells), f32),
            pltpu.VMEM((group * depth_count, PX * PY * slab), f32),
            pltpu.VMEM((group, PX * PY, shells), f32),
            pltpu.SemaphoreType.DMA((2,)),
            pltpu.SemaphoreType.DMA((PX,)),
        ],
        compiler_params=vmem,
        name="assemble",
    )(arrived.reshape(devices, LANES), *radial)
    return smoothed.reshape(1, -1, shells)


def solution(mesh):
    return jax.shard_map(
        on_device,
        mesh=mesh,
        in_specs=(
            P(("depth", "tile")),
            P(("depth", "tile")),
            P(("depth", "tile"), None),
            P(("depth", "tile"), None),
            P(None, ("depth", "tile"), None),
            P(None, ("depth", "tile"), None),
            P(),
            P(),
        ),
        out_specs=P("tile", "depth", None),
        check_vma=False,
    )
```
